32 devices in a mesh: lat: 4 (over z), lon: 8 (over y, x, core).
Axes of the slice: x: 2, y: 2, z: 4, core: 2. Of those that a mesh axis runs over, the one named last changes fastest.
Arguments:
- ensemble: float32 [128, 128, 8, 256], P('lat', 'lon'), may hold values from -6 to 6
- obs_values: float32 [3, 256], replicated, may hold values from -8 to 8
- obs_noise: float32 [3, 256, 256], replicated, may hold values from -6 to 6
- obs_var: float32 [3, 256], replicated, may hold values from 0.1 to 1
- obs_cells: int32 [3, 256], replicated, may hold values from 0 to 4095, as said below
- owner_tiles: int32 [3, 2], replicated, may hold values from 0 to 7, as said below
- radius: int32 [3], replicated, may hold values from 64 to 128, as said below
- courant_lat: float32 [128, 128, 8], P('lat', 'lon'), may hold values from -0.35 to 0.35
- courant_lon: float32 [128, 128, 8], P('lat', 'lon'), may hold values from -0.35 to 0.35
- diffusivity: float32 [128, 128, 8], P('lat', 'lon'), may hold values from 0.02 to 0.07
Outputs:
- forecast: float32 [128, 128, 8, 256], P('lat', 'lon')
The draws below stay inside these ranges and needn't reach their ends.
Inputs may be any that keep to these rules, and one draw needn't show every extreme that they name: `obs_cells`: each row holds 256 distinct local cells, the last cell of the tile among them; cell (i, j, k) of a tile has index (i * 16 + j) * 8 + k. `owner_tiles`: row b names a latitude tile below 4 and a longitude tile below 8; consecutive batches' tiles differ by at most one in each (longitude wraps). `radius`: every draw holds both ends.
All inputs are finite; a program needn't handle non-finite values.
Results may differ from the reference program's by a relative error of at most 0.0003.
Values sent between devices are 32-bit elements; how exact they have to be, the bound alone decides.
No kernel may reach another device: no remote copies, remote signals or barrier semaphores. Data moves between devices by JAX's collectives and lax.ppermute only.
A program may use at most 64 MiB of HBM per device.

```python
import math
import jax
import jax.numpy as jnp
from jax import lax

MEMBERS = 256
LEV = 8
NOBS = 256
NBATCH = 3
CLAT = 32
CLON = 16
NLAT = 128
NLON = 128
RMIN = 64
RMAX = 128


def draw_ensemble(key, part):
    freq_key, coef_key, rough_key, phase_key = jax.random.split(jax.random.fold_in(key, 17), 4)
    mode_count = 24
    frequency = jax.random.uniform(freq_key, (mode_count, 3), jnp.float32, -1.5, 1.5)
    phase_shift = jax.random.uniform(phase_key, (mode_count,), jnp.float32, -3.14159, 3.14159)
    member_coef = jax.random.normal(coef_key, (mode_count, MEMBERS), jnp.float32)
    lat_place = (jnp.arange(NLAT, dtype=jnp.float32) / CLAT)[:, None, None]
    lon_place = (jnp.arange(NLON, dtype=jnp.float32) / CLON)[None, :, None]
    lev_place = (jnp.arange(LEV, dtype=jnp.float32) / LEV)[None, None, :]
    full_shape = (NLAT, NLON, LEV, MEMBERS)
    smooth = jnp.zeros(full_shape, jnp.float32)
    for mode_index in range(mode_count):
        phase_angle = 6.2831853 * (frequency[mode_index, 0] * lat_place + frequency[mode_index, 1] * lon_place + frequency[mode_index, 2] * lev_place) + phase_shift[mode_index]
        amplitude = 0.81 * 0.82 ** mode_index
        smooth = smooth + (amplitude * jnp.sin(phase_angle))[..., None] * member_coef[mode_index]
    rough_part = 0.8 * jax.random.normal(rough_key, full_shape, jnp.float32)
    return jnp.clip(smooth + rough_part, -6.0, 6.0).astype(jnp.float32)


def draw_obs_cells(key, part):
    keys = jax.random.split(jax.random.fold_in(key, 7), NBATCH)
    last_cell = CLAT * CLON * LEV - 1
    picked = []
    for index in range(NBATCH):
        chosen = jax.random.permutation(keys[index], last_cell)[:NOBS - 1]
        picked.append(jnp.concatenate([chosen.astype(jnp.int32), jnp.full((1,), last_cell, jnp.int32)]))
    return jnp.stack(picked).astype(jnp.int32)


def draw_owner_tiles(key, part):
    first_key, second_key, third_key = jax.random.split(jax.random.fold_in(key, 11), 3)
    lon_tiles = NLON // CLON
    lat_anchor = jax.random.randint(first_key, (), 0, NBATCH).astype(jnp.int32)
    lon_anchor = jax.random.randint(second_key, (), 0, NBATCH).astype(jnp.int32)
    moves = jax.random.randint(third_key, (NBATCH, 2), -1, 2).astype(jnp.int32)
    moves = moves.at[0].set(jnp.zeros((2,), jnp.int32))
    walked = jnp.cumsum(moves, axis=0).astype(jnp.int32)
    lat_walk = walked[:, 0]
    lon_walk = walked[:, 1]
    lat_tile = jnp.abs(lat_walk - lat_walk[lat_anchor])
    lon_tile = (lon_tiles - 1 + lon_walk - lon_walk[lon_anchor] + 4 * lon_tiles) % lon_tiles
    return jnp.stack([lat_tile, lon_tile], axis=1).astype(jnp.int32)


def draw_radius(key, part):
    first_key, second_key = jax.random.split(jax.random.fold_in(key, 13), 2)
    middle = jax.random.randint(first_key, (), RMIN, RMAX + 1)
    order = jax.random.permutation(second_key, 3)
    listed = jnp.stack([jnp.asarray(RMAX, jnp.int32), jnp.asarray(RMIN, jnp.int32), middle.astype(jnp.int32)])
    return listed[order].astype(jnp.int32)


def block_scale(stream_key, dims, cuts, smallest, largest):
    def one(dim, shards_of):
        steps = jax.random.uniform(jax.random.fold_in(jax.random.fold_in(stream_key, 6), dim), (shards_of,), jnp.float32, smallest / len(cuts), largest / len(cuts))
        return jnp.repeat(jnp.exp(steps), dims[dim] // shards_of).reshape((-1,) + (1,) * (len(dims) - dim - 1))

    factor_of = one(*cuts[0])
    for cut in cuts[1:]:
        factor_of = factor_of * one(*cut)
    return factor_of


def normal_values(rng, dims, scale, most, kind=jnp.bfloat16):
    drawn = jax.random.normal(rng, dims, jnp.float32) * scale
    return jnp.minimum(jnp.maximum(drawn, -most), most).astype(kind)


def setup_inputs(seed: int = 0) -> dict:
    arg_keys = jax.random.split(jax.random.key(seed), 11)
    return {
        "ensemble": draw_ensemble(jax.random.fold_in(arg_keys[10], 71), 0),
        "obs_values": normal_values(arg_keys[1], (NBATCH, NOBS), 1.5, 8.0, jnp.float32),
        "obs_noise": normal_values(arg_keys[2], (NBATCH, NOBS, MEMBERS), 1.0, 6.0, jnp.float32),
        "obs_var": jnp.clip(jnp.exp(jax.random.uniform(arg_keys[3], (NBATCH, NOBS), jnp.float32, math.log(0.1), math.log(1.0))), 0.1, 1.0),
        "obs_cells": draw_obs_cells(jax.random.fold_in(arg_keys[10], 71), 0),
        "owner_tiles": draw_owner_tiles(jax.random.fold_in(arg_keys[10], 71), 0),
        "radius": draw_radius(jax.random.fold_in(arg_keys[10], 71), 0),
        "courant_lat": jnp.clip(jax.random.uniform(arg_keys[7], (NLAT, NLON, LEV), jnp.float32, -0.35, 0.35) * block_scale(arg_keys[7], (NLAT, NLON, LEV), ((0, 4), (1, 8)), -0.4, 0.0), -0.35, 0.35),
        "courant_lon": jnp.clip(jax.random.uniform(arg_keys[8], (NLAT, NLON, LEV), jnp.float32, -0.35, 0.35) * block_scale(arg_keys[8], (NLAT, NLON, LEV), ((0, 4), (1, 8)), -0.4, 0.0), -0.35, 0.35),
        "diffusivity": jnp.clip(jnp.exp(math.log(0.07) - 1.252763 * jax.random.uniform(arg_keys[9], (NLAT, NLON, LEV), jnp.float32) ** block_scale(arg_keys[9], (NLAT, NLON, LEV), ((0, 4), (1, 8)), -0.2, 0.2)), 0.02, 0.07),
    }


def taper_weight(dist_sq, radius_cells):
    ratio = 1.0 - dist_sq / (radius_cells * radius_cells)
    return jnp.square(jnp.maximum(ratio, 0.0))

def analysis(observed_rows, values, noise, variance):
    members = observed_rows.shape[1]
    spread = observed_rows - lax.optimization_barrier(jnp.mean(observed_rows, axis=1, keepdims=True))
    covariance = jnp.dot(spread, spread.T, precision=lax.Precision.HIGHEST) / (members - 1) + jnp.diag(variance)
    innovation = values[:, None] + jnp.sqrt(variance)[:, None] * noise - observed_rows
    factor = jnp.linalg.cholesky(covariance)
    inner = jax.scipy.linalg.solve_triangular(factor, innovation, lower=True)
    weights = jax.scipy.linalg.solve_triangular(factor, inner, lower=True, trans=1)
    return (spread, weights)

def locality(lat_cells, lon_cells, cells, owner_lat, owner_lon, radius_cells, total_lon):
    position = cells // LEV
    obs_lat = owner_lat * CLAT + position // CLON
    obs_lon = owner_lon * CLON + position % CLON
    lat_gap = (lat_cells[:, None] - obs_lat[None, :]).astype(jnp.float32)
    lon_gap = jnp.abs(lon_cells[:, None] - obs_lon[None, :])
    lon_gap = jnp.minimum(lon_gap, total_lon - lon_gap).astype(jnp.float32)
    dist_sq = jnp.square(lat_gap) + jnp.square(lon_gap)
    return taper_weight(dist_sq, radius_cells.astype(jnp.float32))

def regress(flat_state, spread, weights, weight_map):
    members = flat_state.shape[1]
    places = weight_map.shape[0]
    levels = flat_state.shape[0] // places
    anomaly = flat_state - lax.optimization_barrier(jnp.mean(flat_state, axis=1, keepdims=True))
    covar = jnp.dot(anomaly, spread.T, precision=lax.Precision.HIGHEST) / (members - 1)
    covar = (covar.reshape(places, levels, -1) * weight_map[:, None, :]).reshape(covar.shape)
    return flat_state + jnp.dot(covar, weights, precision=lax.Precision.HIGHEST)

def advance(padded, lat_speed, lon_speed, spread_rate):
    centre = padded[1:-1, 1:-1]
    below_row = padded[:-2, 1:-1]
    above_row = padded[2:, 1:-1]
    west_col = padded[1:-1, :-2]
    east_col = padded[1:-1, 2:]
    lat_part = lat_speed[..., None]
    lon_part = lon_speed[..., None]
    rate_part = spread_rate[..., None]
    transport = jnp.maximum(lat_part, 0.0) * (centre - below_row) + jnp.minimum(lat_part, 0.0) * (above_row - centre) + jnp.maximum(lon_part, 0.0) * (centre - west_col) + jnp.minimum(lon_part, 0.0) * (east_col - centre)
    return centre - transport + rate_part * (below_row + above_row + west_col + east_col - 4.0 * centre)

def pad_global(field):
    padded = jnp.pad(field, ((1, 1), (0, 0), (0, 0)))
    return jnp.concatenate([padded[:, -1:], padded, padded[:, :1]], axis=1)

def reference(ensemble, obs_values, obs_noise, obs_var, obs_cells, owner_tiles, radius, courant_lat, courant_lon, diffusivity):
    nlat_all, nlon_all, levels, members = ensemble.shape
    state = ensemble
    zero_index = jnp.zeros((), jnp.int32)
    for which_batch in range(NBATCH):
        owner_lat = owner_tiles[which_batch, 0]
        owner_lon = owner_tiles[which_batch, 1]
        start_lat = (owner_lat * CLAT).astype(jnp.int32)
        start_lon = (owner_lon * CLON).astype(jnp.int32)
        owner_block = lax.dynamic_slice(state, (start_lat, start_lon, zero_index, zero_index), (CLAT, CLON, levels, members))
        observed_rows = owner_block.reshape(-1, members)[obs_cells[which_batch]]
        spread, weights = analysis(observed_rows, obs_values[which_batch], obs_noise[which_batch], obs_var[which_batch])
        cells = obs_cells[which_batch]
        reach = radius[which_batch]

        def one_row(packed):
            lat_row, lat_number = packed
            lat_cells = jnp.full((nlon_all,), lat_number, jnp.int32)
            lon_cells = jnp.arange(nlon_all, dtype=jnp.int32)
            weight_map = locality(lat_cells, lon_cells, cells, owner_lat, owner_lon, reach, nlon_all)
            return regress(lat_row.reshape(-1, members), spread, weights, weight_map).reshape(lat_row.shape)
        state = lax.map(one_row, (state, jnp.arange(nlat_all, dtype=jnp.int32)))
    by_level = jnp.moveaxis(state, 2, 0)
    coefs = (jnp.moveaxis(courant_lat, 2, 0), jnp.moveaxis(courant_lon, 2, 0), jnp.moveaxis(diffusivity, 2, 0))

    def one_level(packed):
        field, lat_speed, lon_speed, spread_rate = packed
        field = advance(pad_global(field), lat_speed, lon_speed, spread_rate)
        return advance(pad_global(field), lat_speed, lon_speed, spread_rate)
    moved = lax.map(one_level, (by_level,) + coefs)
    return jnp.moveaxis(moved, 0, 2)
```

```python
import functools

import jax
import jax.numpy as jnp
from jax import lax
from jax.experimental import pallas as pl
from jax.experimental.pallas import tpu as pltpu
from jax.sharding import PartitionSpec as P

NBATCH = 3
CLAT = 32
CLON = 16
HALO = 2
F32 = jnp.float32
BF16 = jnp.bfloat16
VMEM = pl.BlockSpec(memory_space=pltpu.VMEM)


def shifted(x, axis, flip):
    size = lax.axis_size(axis)
    return lax.ppermute(x, axis, [(i, i ^ flip) for i in range(size)])


def stages(axis, first):
    size, out = lax.axis_size(axis), []
    while first < size:
        out.append((axis, first))
        first *= 2
    return out


def everywhere(x):
    sizes = (lax.axis_size("lat"), lax.axis_size("lon"))
    if any(n & (n - 1) for n in sizes) or sizes[1] < 2:
        return lax.psum(x, ("lat", "lon"))
    x = x + shifted(x, "lon", 1)
    core = lax.axis_index("lon") % 2
    half = x.shape[0] // 2
    mine = lax.dynamic_slice_in_dim(x, core * half, half, 0)
    a, b = mine[: half // 2], mine[half // 2 :]
    lon, lat = stages("lon", 2), stages("lat", 1)
    for (a_axis, a_flip), (b_axis, b_flip) in zip(lon + lat, lat + lon):
        a, b = a + shifted(a, a_axis, a_flip), b + shifted(b, b_axis, b_flip)
    mine = jnp.concatenate([a, b])
    other = shifted(mine, "lon", 1)
    return jnp.where(
        core == 0, jnp.concatenate([mine, other]), jnp.concatenate([other, mine])
    )


def taper(lat_a, lon_a, lat_b, lon_b, radius, total_lon):
    lat_gap = (lat_a[:, None] - lat_b[None, :]).astype(F32)
    lon_gap = jnp.abs(lon_a[:, None] - lon_b[None, :])
    lon_gap = jnp.minimum(lon_gap, total_lon - lon_gap).astype(F32)
    radius = radius.astype(F32)
    ratio = 1.0 - (jnp.square(lat_gap) + jnp.square(lon_gap)) / (radius * radius)
    return jnp.square(jnp.maximum(ratio, 0.0))


def split(x):
    high = x.astype(BF16)
    return high, (x - high.astype(F32)).astype(BF16)


def exact_dot(a, b):
    return jnp.dot(a, b, precision=lax.Precision.HIGHEST, preferred_element_type=F32)


def split_dot(a, b_high, *b_rest):
    high, low = split(a)
    dot = functools.partial(jnp.dot, preferred_element_type=F32)
    total = dot(high, b_high) + dot(low, b_high)
    for b in b_rest:
        total = total + dot(high, b)
    return total


def eliminate(strips):
    shape = strips[0].shape
    lane = lax.broadcasted_iota(jnp.int32, shape, 1)
    row = lax.broadcasted_iota(jnp.int32, shape, 0)
    block = lane < 8
    first = strips[0]
    diag = [jnp.broadcast_to(first[:, c : c + 1], shape) for c in range(8)]
    scaled = jnp.where(block, jnp.where(lane == row, 1.0, 0.0), first)
    for k in range(8):
        pivot = 1.0 / jnp.broadcast_to(diag[k][k : k + 1], shape)
        here = row == k
        for c in range(k + 1, 8):
            top = jnp.broadcast_to(diag[c][k : k + 1], shape) * pivot
            diag[c] = jnp.where(here, top, diag[c] - diag[k] * top)
        top = jnp.broadcast_to(scaled[k : k + 1], shape) * pivot
        scaled = jnp.where(here, top, scaled - diag[k] * top)
    rows = [jnp.broadcast_to(scaled[c : c + 1], shape) for c in range(8)]
    out = []
    for strip in strips[1:]:
        terms = [jnp.broadcast_to(strip[:, c : c + 1], shape) * rows[c] for c in range(8)]
        while len(terms) > 1:
            terms = [terms[j] + terms[j + 1] for j in range(0, len(terms), 2)]
        out.append(jnp.where(block, 0.0, strip) - terms[0])
    out.append(scaled)
    return tuple(pltpu.roll(strip, shape[1] - 8, 1) for strip in out)


def inverse(a):
    size = a.shape[0]
    strips = tuple(a[8 * i : 8 * i + 8] for i in range(size // 8))
    strips = lax.fori_loop(0, size // 8, lambda _, s: eliminate(s), strips)
    return jnp.concatenate(strips, axis=0)


def solve_kernel(
    rows_ref, target_ref, var_ref, mutual_ref, st_high, st_low, w_high, w_mid, w_low, y_ref
):
    count, nobs, members = rows_ref.shape
    half = nobs // 2
    y_ref[...] = rows_ref[...]
    diagonal = lax.broadcasted_iota(jnp.int32, (nobs, nobs), 0) == lax.broadcasted_iota(
        jnp.int32, (nobs, nobs), 1
    )

    @pl.loop(0, count)
    def _(b):
        y = y_ref[b]
        spread = y - jnp.sum(y, axis=1, keepdims=True) / members
        spread_t = spread.T
        high, low = split(spread_t)
        st_high[b] = high
        st_low[b] = low
        cov = exact_dot(spread, spread_t) / (members - 1)
        cov = cov + jnp.where(diagonal, jnp.broadcast_to(var_ref[b], (nobs, nobs)), 0.0)
        right = target_ref[b] - y
        lower = cov[half:, :half]
        upper = jnp.concatenate([cov[:half, half:], right[:half]], axis=1)
        upper = exact_dot(inverse(cov[:half, :half]), upper)
        rest = exact_dot(lower, upper)
        schur = inverse(cov[half:, half:] - rest[:, :half])
        w_second = exact_dot(schur, right[half:] - rest[:, half:])
        w_first = upper[:, half:] - exact_dot(upper[:, :half], w_second)
        w = jnp.concatenate([w_first, w_second], axis=0)
        high, mid = split(w)
        w_high[b] = high
        w_mid[b] = mid
        w_low[b] = (w - high.astype(F32) - mid.astype(F32)).astype(BF16)

        @pl.loop(b + 1, count)
        def _(later):
            y_later = y_ref[later]
            gain = exact_dot(y_later, spread_t) * mutual_ref[b + later - 1]
            y_ref[later] = y_later + exact_dot(gain, w)


def solve(rows, target, variance, mutual):
    count, nobs, members = rows.shape
    out = [jax.ShapeDtypeStruct((count, members, nobs), BF16)] * 2
    out += [jax.ShapeDtypeStruct((count, nobs, members), BF16)] * 3
    return pl.pallas_call(
        solve_kernel,
        out_shape=out,
        in_specs=[VMEM] * 4,
        out_specs=[VMEM] * 5,
        scratch_shapes=[pltpu.VMEM((count, nobs, members), F32)],
        compiler_params=pltpu.CompilerParams(vmem_limit_bytes=60 << 20),
    )(rows, target, variance[:, None, :], mutual)


def sweep(source, coef_ref, i, width, coef_row, coef_col, store):
    rows = [[source[i + d, j] for j in range(width + 2)] if d == 1 else None for d in range(3)]
    for j in range(width):
        near = (rows[1][j + 1], source[i, j + 1], source[i + 2, j + 1], rows[1][j], rows[1][j + 2])
        total = None
        for n, part in enumerate(near):
            coef = coef_ref[n, coef_row, coef_col + j]
            coef = jnp.concatenate([coef] * (part.shape[-1] // coef.shape[-1]), axis=-1)
            total = part * coef if total is None else total + part * coef
        store(j, total)


def move_kernel(chunk, *refs):
    pieces, refs = refs[:5], refs[5:]
    taper_hbm, coef_hbm, st_high, st_low, w_high, w_mid, w_low = refs[:7]
    out_hbm, x_ref, taper_ref, coef_ref, z_ref, out_ref, sems, out_sem = refs[7:]
    count = st_high.shape[0]
    tall, wide, levels, members = x_ref.shape
    inner = (pl.ds(HALO, tall - 2 * HALO), pl.ds(HALO, wide - 2 * HALO))
    places = (
        inner,
        (pl.ds(0, HALO), inner[1]),
        (pl.ds(tall - HALO, HALO), inner[1]),
        (slice(None), pl.ds(0, HALO)),
        (slice(None), pl.ds(wide - HALO, HALO)),
    )
    copies = [
        pltpu.make_async_copy(piece, x_ref.at[place], sems.at[n])
        for n, (piece, place) in enumerate(zip(pieces, places))
    ]
    copies.append(pltpu.make_async_copy(taper_hbm, taper_ref, sems.at[5]))
    coef_copy = pltpu.make_async_copy(coef_hbm, coef_ref, sems.at[6])
    for copy in copies:
        copy.start()
    coef_copy.start()
    for copy in copies:
        copy.wait()

    @pl.loop(0, tall // chunk)
    def _(i):
        at = pl.ds(i * chunk, chunk)
        x = x_ref[at].reshape(chunk * wide * levels, members)
        for b in range(count):
            gain = split_dot(x, st_high[b], st_low[b]).reshape(chunk * wide, levels, -1)
            gain = gain * taper_ref[b, at].reshape(chunk * wide, -1)[:, None, :]
            gain = gain.reshape(chunk * wide * levels, -1)
            x = x + split_dot(gain, w_high[b], w_mid[b], w_low[b])
        x_ref[at] = x.reshape(chunk, wide, levels, members)

    coef_copy.wait()

    @pl.loop(0, tall - 2)
    def _(i):
        def store(j, value):
            z_ref[i, j] = value

        sweep(x_ref, coef_ref, i, wide - 2, i + 1, 1, store)

    @pl.loop(0, tall - 4)
    def _(i):
        def store(j, value):
            out_ref[i, j] = value

        sweep(z_ref, coef_ref, i, wide - 4, i + 2, 2, store)
        pltpu.make_async_copy(out_ref.at[i], out_hbm.at[i], out_sem).start()

    pltpu.make_async_copy(out_ref, out_hbm, out_sem).wait()


def move(pieces, tapers, coefs, spread_t, weights):
    wide, (tall, _, levels, members) = pieces[0].shape[1] + 2 * HALO, pieces[3].shape
    hbm = pl.BlockSpec(memory_space=pl.ANY)
    return pl.pallas_call(
        functools.partial(move_kernel, 4 if tall % 4 == 0 else 1),
        out_shape=jax.ShapeDtypeStruct(pieces[0].shape, F32),
        in_specs=[hbm] * 7 + [VMEM] * 5,
        out_specs=hbm,
        scratch_shapes=[
            pltpu.VMEM((tall, wide, levels, members), F32),
            pltpu.VMEM(tapers.shape, F32),
            pltpu.VMEM(coefs.shape, F32),
            pltpu.VMEM((tall - 2, wide - 2, levels, members), F32),
            pltpu.VMEM(pieces[0].shape, F32),
            pltpu.SemaphoreType.DMA((7,)),
            pltpu.SemaphoreType.DMA,
        ],
        compiler_params=pltpu.CompilerParams(vmem_limit_bytes=60 << 20),
    )(*pieces, tapers, coefs, *spread_t, *weights)


def packed(x, extra):
    width = x.shape[-1]
    extra = extra.reshape(-1)
    tail = -(-extra.shape[0] // (8 * width)) * 8
    extra = jnp.pad(extra, (0, tail * width - extra.shape[0])).reshape(tail, width)
    return jnp.concatenate([x.reshape(-1, width), extra])


def unpacked(rows, shape, extra_shape):
    count = 1
    for n in shape[:-1]:
        count *= n
    size = 1
    for n in extra_shape:
        size *= n
    return rows[:count].reshape(shape), rows[count:].reshape(-1)[:size].reshape(extra_shape)


def edges(x, extra, axis, dim, wrap):
    size, length = lax.axis_size(axis), x.shape[dim]
    up = [(i, (i + 1) % size) for i in range(size if wrap else size - 1)]
    down = [(j, i) for i, j in up]
    found = []
    for pairs, at in ((up, length - HALO), (down, 0)):
        edge = lax.slice_in_dim(x, at, at + HALO, axis=dim)
        last = extra.shape[dim + 1] - 1 if at else 0
        thin = lax.slice_in_dim(extra, last, last + 1, axis=dim + 1)
        got = lax.ppermute(packed(edge, thin), axis, pairs)
        found.append(unpacked(got, edge.shape, thin.shape))
    return found


def shards(
    ensemble,
    obs_values,
    obs_noise,
    obs_var,
    obs_cells,
    owner_tiles,
    radius,
    courant_lat,
    courant_lon,
    diffusivity,
):
    lat_index = lax.axis_index("lat")
    lon_index = lax.axis_index("lon")
    total_lon = CLON * lax.axis_size("lon")
    levels, members = ensemble.shape[2:]
    nobs = obs_cells.shape[1]

    mine = jnp.logical_and(owner_tiles[:, 0] == lat_index, owner_tiles[:, 1] == lon_index)
    rows = ensemble.reshape(-1, members)[obs_cells.reshape(-1)]
    rows = jnp.where(jnp.repeat(mine, nobs)[:, None], rows, 0.0)
    rows = everywhere(rows).reshape(NBATCH, nobs, members)

    stacked = jnp.stack([courant_lat, courant_lon, diffusivity])
    (south, south_thin), (north, north_thin) = edges(ensemble, stacked, "lat", 0, False)
    rows, south, north = lax.optimization_barrier((rows, south, north))
    stacked = jnp.concatenate([south_thin, stacked, north_thin], axis=1)
    columns = jnp.concatenate(
        [
            jnp.concatenate([part[:, :HALO], part[:, -HALO:]], axis=1)
            for part in (south, ensemble, north)
        ]
    )
    (west, west_thin), (east, east_thin) = edges(columns, stacked, "lon", 1, True)
    stacked = jnp.concatenate([west_thin, stacked, east_thin], axis=2)
    tall, wide = west.shape[0], ensemble.shape[1] + 2 * HALO
    stacked = jnp.pad(stacked, ((0, 0), (1, 1), (1, 1), (0, 0)))
    lat_speed, lon_speed, rate = stacked
    coefs = jnp.stack(
        [
            1.0 - jnp.abs(lat_speed) - jnp.abs(lon_speed) - 4.0 * rate,
            jnp.maximum(lat_speed, 0.0) + rate,
            rate - jnp.minimum(lat_speed, 0.0),
            jnp.maximum(lon_speed, 0.0) + rate,
            rate - jnp.minimum(lon_speed, 0.0),
        ]
    )
    coefs = jnp.broadcast_to(coefs[..., None], coefs.shape + (128,))

    place = obs_cells // levels
    obs_lat = owner_tiles[:, :1] * CLAT + place // CLON
    obs_lon = owner_tiles[:, 1:] * CLON + place % CLON
    lat_cells = lat_index * CLAT - HALO + jnp.arange(tall, dtype=jnp.int32)
    lon_cells = lon_index * CLON - HALO + jnp.arange(wide, dtype=jnp.int32)
    lon_cells = (lon_cells + total_lon) % total_lon
    lat_cells = jnp.broadcast_to(lat_cells[:, None], (tall, wide)).reshape(-1)
    lon_cells = jnp.broadcast_to(lon_cells[None, :], (tall, wide)).reshape(-1)
    tapers = jnp.stack(
        [
            taper(lat_cells, lon_cells, obs_lat[b], obs_lon[b], radius[b], total_lon)
            for b in range(NBATCH)
        ]
    ).reshape(NBATCH, tall, wide, nobs) / (members - 1)
    mutual = jnp.stack(
        [
            taper(obs_lat[c], obs_lon[c], obs_lat[b], obs_lon[b], radius[b], total_lon)
            for b, c in ((0, 1), (0, 2), (1, 2))
        ]
    ) / (members - 1)
    target = obs_values[:, :, None] + jnp.sqrt(obs_var)[:, :, None] * obs_noise

    factors = solve(rows, target, obs_var, mutual)
    pieces = (ensemble, south, north, west, east)
    return move(pieces, tapers, coefs, factors[:2], factors[2:])


def solution(mesh):
    cells = P("lat", "lon", None)
    in_specs = (P("lat", "lon", None, None),) + (P(),) * 6 + (cells,) * 3
    out_specs = P("lat", "lon", None, None)
    return jax.shard_map(
        shards, mesh=mesh, in_specs=in_specs, out_specs=out_specs, check_vma=False
    )
```

```python
import functools

import jax
import jax.numpy as jnp
from jax import lax
from jax.experimental import pallas as pl
from jax.experimental.pallas import tpu as pltpu
from jax.sharding import PartitionSpec as P

NBATCH = 3
CLAT = 32
CLON = 16
HALO = 2
LANES = 128
F32 = jnp.float32
BF16 = jnp.bfloat16
VMEM = pl.BlockSpec(memory_space=pltpu.VMEM)


def shifted(x, axis, flip):
    size = lax.axis_size(axis)
    return lax.ppermute(x, axis, [(i, i ^ flip) for i in range(size)])


def stages(axis, first):
    size, out = lax.axis_size(axis), []
    while first < size:
        out.append((axis, first))
        first *= 2
    return out


def gather_kernel(cells, tiles, spot, state_hbm, first_ref, second_ref, state_ref, sem):
    count, half, members = first_ref.shape
    core = lax.rem(spot[1], 2)

    def owned(b):
        return jnp.logical_and(tiles[b, 0] == spot[0], tiles[b, 1] == spot[1])

    any_owned = owned(0)
    for b in range(1, count):
        any_owned = jnp.logical_or(any_owned, owned(b))

    @pl.when(any_owned)
    def _():
        copy = pltpu.make_async_copy(state_hbm, state_ref, sem)
        copy.start()
        copy.wait()

    for b in range(count):
        mine = owned(b)
        for side, ref in enumerate((first_ref, second_ref)):
            start = lax.rem(core + side, 2) * half

            @pl.when(mine)
            def _():
                @pl.loop(0, half // 8)
                def _(i):
                    for n in range(8):
                        row = state_ref[pl.ds(cells[b, start + i * 8 + n], 1), :]
                        ref[b, pl.ds(i * 8 + n, 1), :] = row

            @pl.when(jnp.logical_not(mine))
            def _():
                ref[b] = jnp.zeros((half, members), F32)


def gather(ensemble, cells, tiles, spot):
    members = ensemble.shape[-1]
    flat = ensemble.reshape(-1, members)
    count, nobs = cells.shape
    smem = pl.BlockSpec(memory_space=pltpu.SMEM)
    out = jax.ShapeDtypeStruct((count, nobs // 2, members), F32)
    return pl.pallas_call(
        gather_kernel,
        out_shape=[out, out],
        in_specs=[smem] * 3 + [pl.BlockSpec(memory_space=pl.ANY)],
        out_specs=[VMEM] * 2,
        scratch_shapes=[pltpu.VMEM(flat.shape, F32), pltpu.SemaphoreType.DMA],
        compiler_params=pltpu.CompilerParams(vmem_limit_bytes=24 << 20),
    )(cells, tiles, spot, flat)


def spread_out(mine, half, fillers):
    fillers, made = list(fillers), []
    a, b = mine[:, :half], mine[:, half:]
    lon, lat = stages("lon", 2), stages("lat", 1)
    for (a_axis, a_flip), (b_axis, b_flip) in zip(lon + lat, lat + lon):
        a_moved, b_moved = shifted(a, a_axis, a_flip), shifted(b, b_axis, b_flip)
        a, b = a + a_moved, b + b_moved
        if fillers:
            a, b, filler = lax.optimization_barrier((a, b, fillers.pop(0)))
            made.append(filler)
    return (a, b, shifted(a, "lon", 1), shifted(b, "lon", 1)), made + fillers


def taper(lat_a, lon_a, lat_b, lon_b, radius, total_lon):
    lat_gap = (lat_a[:, None] - lat_b[None, :]).astype(F32)
    lon_gap = jnp.abs(lon_a[:, None] - lon_b[None, :])
    lon_gap = jnp.minimum(lon_gap, total_lon - lon_gap).astype(F32)
    radius = radius.astype(F32)
    ratio = 1.0 - (jnp.square(lat_gap) + jnp.square(lon_gap)) / (radius * radius)
    return jnp.square(jnp.maximum(ratio, 0.0))


def split(x):
    high = x.astype(BF16)
    return high, (x - high.astype(F32)).astype(BF16)


def exact_dot(a, b):
    return jnp.dot(a, b, precision=lax.Precision.HIGHEST, preferred_element_type=F32)


def split_dot(a, b_high, *b_rest):
    high, low = split(a)
    dot = functools.partial(jnp.dot, preferred_element_type=F32)
    total = dot(high, b_high) + dot(low, b_high)
    for b in b_rest:
        total = total + dot(high, b)
    return total


def lane_spread(x, lane):
    return jnp.take_along_axis(x, jnp.full(x.shape, lane, jnp.int32), axis=1)


def panel(strips):
    strips, shape = list(strips), strips[0].shape
    lane = lax.broadcasted_iota(jnp.int32, shape, 1)
    row = lax.broadcasted_iota(jnp.int32, shape, 0)
    for g, first in enumerate(strips):
        at = 8 * g
        block = jnp.logical_and(lane >= at, lane < at + 8)
        first = strips[g]
        diag = [lane_spread(first, at + c) for c in range(8)]
        left = {
            h: [lane_spread(strip, at + c) for c in range(8)]
            for h, strip in enumerate(strips)
            if h != g
        }
        scaled = jnp.where(block, jnp.where(lane == row + at, 1.0, 0.0), first)
        for k in range(0, 8, 2):

            def pick(x, n):
                return jnp.broadcast_to(x[n : n + 1], shape)

            p, q, r = pick(diag[k], k), pick(diag[k], k + 1), pick(diag[k + 1], k + 1)
            pivot = 1.0 / (p * r - q * q)

            def reduced(x):
                upper, lower = pick(x, k), pick(x, k + 1)
                upper, lower = (r * upper - q * lower) * pivot, (p * lower - q * upper) * pivot
                x = x - (diag[k] * upper + diag[k + 1] * lower)
                return jnp.where(row == k, upper, jnp.where(row == k + 1, lower, x))

            diag[k + 2 :] = [reduced(x) for x in diag[k + 2 :]]
            scaled = reduced(scaled)
        rows = [jnp.broadcast_to(scaled[c : c + 1], shape) for c in range(8)]
        for h, columns in left.items():
            terms = [columns[c] * rows[c] for c in range(8)]
            while len(terms) > 1:
                terms = [terms[j] + terms[j + 1] for j in range(0, len(terms), 2)]
            strips[h] = jnp.where(block, 0.0, strips[h]) - terms[0]
        strips[g] = scaled
    return strips


def inverse(a, block=64):
    size = a.shape[0]

    def turn(_, a):
        top = panel([a[8 * i : 8 * i + 8] for i in range(block // 8)])
        top, rest = jnp.concatenate(top), a[block:]
        lane = lax.broadcasted_iota(jnp.int32, rest.shape, 1)
        rest = jnp.where(lane < block, 0.0, rest) - exact_dot(rest[:, :block], top)
        return pltpu.roll(jnp.concatenate([rest, top]), size - block, 1)

    return lax.fori_loop(0, size // block, turn, a)


def solve_kernel(*refs):
    pieces, refs = refs[:4], refs[4:]
    target_ref, var_ref, mutual_ref, out_hbm, y_ref, out_ref, sem = refs
    count, nobs, members = target_ref.shape
    half = nobs // 2
    for n, piece in enumerate(pieces):
        size = piece.shape[1]
        y_ref[:, n * size : (n + 1) * size] = piece[...]
    diagonal = lax.broadcasted_iota(jnp.int32, (nobs, nobs), 0) == lax.broadcasted_iota(
        jnp.int32, (nobs, nobs), 1
    )

    @pl.loop(0, count)
    def _(b):
        y = y_ref[b]
        spread = y - jnp.sum(y, axis=1, keepdims=True) / members
        spread_t = spread.T
        out_ref[b, 0], out_ref[b, 1] = split(spread_t)
        cov = exact_dot(spread, spread_t) / (members - 1)
        cov = cov + jnp.where(diagonal, jnp.broadcast_to(var_ref[b], (nobs, nobs)), 0.0)
        right = target_ref[b] - y
        lower = cov[half:, :half]
        upper = jnp.concatenate([cov[:half, half:], right[:half]], axis=1)
        upper = exact_dot(inverse(cov[:half, :half]), upper)
        rest = exact_dot(lower, upper)
        schur = inverse(cov[half:, half:] - rest[:, :half])
        w_second = exact_dot(schur, right[half:] - rest[:, half:])
        w_first = upper[:, half:] - exact_dot(upper[:, :half], w_second)
        w = jnp.concatenate([w_first, w_second], axis=0)
        high, mid = split(w)
        out_ref[b, 2] = high
        out_ref[b, 3] = mid
        out_ref[b, 4] = (w - high.astype(F32) - mid.astype(F32)).astype(BF16)
        pltpu.make_async_copy(out_ref.at[b], out_hbm.at[b], sem).start()

        @pl.loop(b + 1, count)
        def _(later):
            y_later = y_ref[later]
            gain = exact_dot(y_later, spread_t) * mutual_ref[b + later - 1]
            y_ref[later] = y_later + exact_dot(gain, w)

    pltpu.make_async_copy(out_ref, out_hbm, sem).wait()


def solve(pieces, target, variance, mutual):
    count, nobs, members = target.shape
    out = (count, 5, nobs, members)
    return pl.pallas_call(
        solve_kernel,
        out_shape=jax.ShapeDtypeStruct(out, BF16),
        in_specs=[VMEM] * 7,
        out_specs=pl.BlockSpec(memory_space=pl.ANY),
        scratch_shapes=[
            pltpu.VMEM((count, nobs, members), F32),
            pltpu.VMEM(out, BF16),
            pltpu.SemaphoreType.DMA,
        ],
        compiler_params=pltpu.CompilerParams(vmem_limit_bytes=40 << 20),
        cost_estimate=pl.CostEstimate(
            flops=60 * count * nobs**3, bytes_accessed=4 * 8 * target.size, transcendentals=0
        ),
    )(*pieces, target, variance[:, None, :], mutual)


def sweep(source, j, height, coef_at, store):
    middle = [source[i, j + 1] for i in range(height + 2)]
    for i in range(height):
        near = (middle[i + 1], middle[i], middle[i + 2], source[i + 1, j], source[i + 1, j + 2])
        total = None
        for coef, part in zip(coef_at(i), near):
            coef = jnp.concatenate([coef] * (part.shape[-1] // coef.shape[-1]), axis=-1)
            total = part * coef if total is None else total + part * coef
        store(i, total)


def five(lat_speed, lon_speed, rate):
    return (
        1.0 - jnp.abs(lat_speed) - jnp.abs(lon_speed) - 4.0 * rate,
        jnp.maximum(lat_speed, 0.0) + rate,
        rate - jnp.minimum(lat_speed, 0.0),
        jnp.maximum(lon_speed, 0.0) + rate,
        rate - jnp.minimum(lon_speed, 0.0),
    )


def move_kernel(chunk, *refs):
    pieces, refs = refs[:5], refs[5:]
    taper_hbm, coef_hbm, factor_hbm, out_hbm, x_ref, taper_ref, factor_ref = refs[:7]
    coef_ref, wide_ref, z_ref, out_ref, sems, out_sem = refs[7:]
    count = factor_ref.shape[0]
    tall, wide, levels, members = x_ref.shape
    inner = (pl.ds(HALO, tall - 2 * HALO), pl.ds(HALO, wide - 2 * HALO))
    places = (
        inner,
        (pl.ds(0, HALO), inner[1]),
        (pl.ds(tall - HALO, HALO), inner[1]),
        (slice(None), pl.ds(0, HALO)),
        (slice(None), pl.ds(wide - HALO, HALO)),
    )
    heights = (tall - 2 * HALO, HALO, HALO, tall, tall)
    copies = [
        pltpu.make_async_copy(piece.at[pl.ds(0, height)], x_ref.at[place], sems.at[n])
        for n, (piece, place, height) in enumerate(zip(pieces, places, heights))
    ]
    copies.append(pltpu.make_async_copy(taper_hbm, taper_ref, sems.at[5]))
    copies.append(pltpu.make_async_copy(factor_hbm, factor_ref, sems.at[13]))
    coef_copies = [
        pltpu.make_async_copy(coef_hbm, coef_ref.at[:, pl.ds(1, wide - 4)], sems.at[6])
    ]
    for n in range(3):
        for side in range(2):
            source = pieces[3 + side].at[tall + n // 2, n % 2, :, pl.ds(0, coef_ref.shape[-1])]
            to = coef_ref.at[n, side * (wide - 3)]
            coef_copies.append(pltpu.make_async_copy(source, to, sems.at[7 + 2 * n + side]))
    for copy in copies + coef_copies:
        copy.start()
    for copy in copies:
        copy.wait()

    @pl.loop(0, tall // chunk)
    def _(i):
        at = pl.ds(i * chunk, chunk)
        x = x_ref[at].reshape(chunk * wide * levels, members)
        for b in range(count):
            gain = split_dot(x, factor_ref[b, 0], factor_ref[b, 1])
            gain = gain.reshape(chunk * wide, levels, -1)
            gain = gain * taper_ref[b, at].reshape(chunk * wide, -1)[:, None, :]
            gain = gain.reshape(chunk * wide * levels, -1)
            x = x + split_dot(gain, factor_ref[b, 2], factor_ref[b, 3], factor_ref[b, 4])
        x_ref[at] = x.reshape(chunk, wide, levels, members)

    for copy in coef_copies:
        copy.wait()

    @pl.loop(0, wide - 2)
    def _(j):
        tiles = five(*[coef_ref[n, j] for n in range(3)])

        def coef_at(i):
            found = [jnp.broadcast_to(tile[:, i : i + 1], (levels, LANES)) for tile in tiles]
            for n, coef in enumerate(found):
                wide_ref[n, i, j] = coef
            return found

        def store(i, value):
            z_ref[i, j] = value

        sweep(x_ref, j, tall - 2, coef_at, store)

    @pl.loop(0, wide - 4)
    def _(j):
        def store(i, value):
            out_ref[i, j] = value

        def coef_at(i):
            return [wide_ref[n, i + 1, j + 1] for n in range(5)]

        sweep(z_ref, j, tall - 4, coef_at, store)
        pltpu.make_async_copy(out_ref.at[:, j], out_hbm.at[:, j], out_sem).start()

    pltpu.make_async_copy(out_ref, out_hbm, out_sem).wait()


def move(pieces, tapers, coefs, factors):
    tall, wide = pieces[0].shape[0] + 2 * HALO, pieces[0].shape[1] + 2 * HALO
    levels, members = pieces[0].shape[2:]
    hbm = pl.BlockSpec(memory_space=pl.ANY)
    return pl.pallas_call(
        functools.partial(move_kernel, 12 if tall % 12 == 0 else 1),
        out_shape=jax.ShapeDtypeStruct(pieces[0].shape, F32),
        in_specs=[hbm] * 8,
        out_specs=hbm,
        scratch_shapes=[
            pltpu.VMEM((tall, wide, levels, members), F32),
            pltpu.VMEM(tapers.shape, F32),
            pltpu.VMEM(factors.shape, BF16),
            pltpu.VMEM((3, wide - 2, levels, coefs.shape[-1]), F32),
            pltpu.VMEM((5, tall - 2, wide - 2, levels, LANES), F32),
            pltpu.VMEM((tall - 2, wide - 2, levels, members), F32),
            pltpu.VMEM(pieces[0].shape, F32),
            pltpu.SemaphoreType.DMA((14,)),
            pltpu.SemaphoreType.DMA,
        ],
        compiler_params=pltpu.CompilerParams(vmem_limit_bytes=60 << 20),
    )(*pieces, tapers, coefs, factors)


def lanes(x, count):
    return jnp.pad(x, [(0, 0)] * (x.ndim - 1) + [(0, count - x.shape[-1])])


def neighbours(before, after, axis, wrap):
    size = lax.axis_size(axis)
    up = [(i, (i + 1) % size) for i in range(size if wrap else size - 1)]
    down = [(j, i) for i, j in up]
    return lax.ppermute(before, axis, up), lax.ppermute(after, axis, down)


def shards(
    ensemble,
    obs_values,
    obs_noise,
    obs_var,
    obs_cells,
    owner_tiles,
    radius,
    courant_lat,
    courant_lon,
    diffusivity,
):
    lat_index = lax.axis_index("lat")
    lon_index = lax.axis_index("lon")
    total_lon = CLON * lax.axis_size("lon")
    levels, members = ensemble.shape[2:]
    nobs = obs_cells.shape[1]

    core = lon_index % 2
    half = nobs // 2
    spot = jnp.stack([lat_index, lon_index])
    mine, others = gather(ensemble, obs_cells, owner_tiles, spot)
    mine = mine + shifted(others, "lon", 1)
    (
        mine,
        obs_cells,
        obs_values,
        obs_var,
        obs_noise,
        owner_tiles,
        radius,
        courant_lat,
        courant_lon,
        diffusivity,
        south,
        north,
    ) = lax.optimization_barrier(
        (
            mine,
            obs_cells,
            obs_values,
            obs_var,
            obs_noise,
            owner_tiles,
            radius,
            courant_lat,
            courant_lon,
            diffusivity,
            ensemble[-HALO:],
            ensemble[:HALO],
        )
    )

    def own_first(x):
        x = jnp.concatenate([x, x[:, :half]], axis=1)
        return lax.dynamic_slice_in_dim(x, core * half, nobs, 1)

    obs_cells, obs_values, obs_var, obs_noise = map(
        own_first, (obs_cells, obs_values, obs_var, obs_noise)
    )

    speeds = jnp.stack([courant_lat, courant_lon, diffusivity]).transpose(0, 2, 3, 1)
    thin = lanes(speeds[..., -1:].transpose(3, 1, 2, 0), members)
    south = jnp.concatenate([south, thin])
    thin = lanes(speeds[..., :1].transpose(3, 1, 2, 0), members)
    north = jnp.concatenate([north, thin])
    south, north = neighbours(south, north, "lat", False)
    south_thin, north_thin = (
        side[HALO:, :, :, :3].transpose(3, 1, 2, 0) for side in (south, north)
    )
    speeds = jnp.concatenate([south_thin, speeds, north_thin], axis=-1)
    speeds = lanes(speeds, LANES)

    tall, wide = ensemble.shape[0] + 2 * HALO, ensemble.shape[1] + 2 * HALO
    place = obs_cells // levels
    obs_lat = owner_tiles[:, :1] * CLAT + place // CLON
    obs_lon = owner_tiles[:, 1:] * CLON + place % CLON
    lat_cells = lat_index * CLAT - HALO + jnp.arange(tall, dtype=jnp.int32)
    lon_cells = lon_index * CLON - HALO + jnp.arange(wide, dtype=jnp.int32)
    lon_cells = (lon_cells + total_lon) % total_lon
    lat_cells = jnp.broadcast_to(lat_cells[:, None], (tall, wide)).reshape(-1)
    lon_cells = jnp.broadcast_to(lon_cells[None, :], (tall, wide)).reshape(-1)
    tapers = jnp.stack(
        [
            taper(lat_cells, lon_cells, obs_lat[b], obs_lon[b], radius[b], total_lon)
            for b in range(NBATCH)
        ]
    ).reshape(NBATCH, tall, wide, nobs) / (members - 1)
    mutual = jnp.stack(
        [
            taper(obs_lat[c], obs_lon[c], obs_lat[b], obs_lon[b], radius[b], total_lon)
            for b, c in ((0, 1), (0, 2), (1, 2))
        ]
    ) / (members - 1)
    target = obs_values[:, :, None] + jnp.sqrt(obs_var)[:, :, None] * obs_noise

    def side(at, extent, lane):
        edge = jnp.concatenate([part[:, at:extent] for part in (south[:HALO], ensemble, north[:HALO])])
        tile = lanes(speeds[:, lane], members)
        tile = jnp.pad(tile, ((0, 1), (0, 0), (0, 0))).reshape((2, 2) + tile.shape[1:])
        return jnp.concatenate([edge, tile])

    last = ensemble.shape[1]
    before, after = side(last - HALO, last, last - 1), side(0, HALO, 0)
    pieces, (tapers, (target, mutual), (speeds, before, after)) = spread_out(
        mine, half // 2, (tapers, (target, mutual), (speeds, before, after))
    )
    pieces, before, after = lax.optimization_barrier((pieces, before, after))
    west, east = neighbours(before, after, "lon", True)
    factors = solve(pieces, target, obs_var, mutual)
    cells = (ensemble, south, north, west, east)
    return move(cells, tapers, speeds, factors)


def solution(mesh):
    cells = P("lat", "lon", None)
    in_specs = (P("lat", "lon", None, None),) + (P(),) * 6 + (cells,) * 3
    out_specs = P("lat", "lon", None, None)
    return jax.shard_map(
        shards, mesh=mesh, in_specs=in_specs, out_specs=out_specs, check_vma=False
    )
```

```python
import functools

import jax
import jax.numpy as jnp
from jax import lax
from jax.experimental import pallas as pl
from jax.experimental.pallas import tpu as pltpu
from jax.sharding import PartitionSpec as P

NBATCH = 3
CLAT = 32
CLON = 16
HALO = 2
LANES = 128
F32 = jnp.float32
BF16 = jnp.bfloat16
VMEM = pl.BlockSpec(memory_space=pltpu.VMEM)
HBM = pl.BlockSpec(memory_space=pltpu.HBM)


def in_hbm(x):
    return pltpu.with_memory_space_constraint(x, pltpu.HBM)


def shifted(x, axis, flip):
    size = lax.axis_size(axis)
    return lax.ppermute(x, axis, [(i, i ^ flip) for i in range(size)])


def stages(axis, first):
    size, out = lax.axis_size(axis), []
    while first < size:
        out.append((axis, first))
        first *= 2
    return out


def gather_kernel(cells_hbm, tiles_hbm, state_hbm, *refs):
    first_ref, second_ref, cells, tiles, state_ref, sems = refs
    pairs = ((tiles_hbm, tiles), (cells_hbm, cells), (state_hbm, state_ref))
    copies = [pltpu.make_async_copy(x, to, sems.at[n]) for n, (x, to) in enumerate(pairs)]
    for copy in copies:
        copy.start()
    parts, count, rows, members = first_ref.shape
    lat, lon = lax.axis_index("lat"), lax.axis_index("lon")
    core = lax.rem(lon, 2)
    first_ref[...] = jnp.zeros(first_ref.shape, F32)
    second_ref[...] = jnp.zeros(second_ref.shape, F32)
    for copy in copies:
        copy.wait()
    for b in range(count):

        @pl.when(jnp.logical_and(tiles[0, b] == lat, tiles[1, b] == lon))
        def _():
            for side, ref in enumerate((first_ref, second_ref)):
                for part in range(parts):
                    start = (lax.rem(core + side, 2) * parts + part) * rows

                    @pl.loop(0, rows // 8)
                    def _(i):
                        for n in range(8):
                            cell = cells[b, start + i * 8 + n]
                            ref[part, b, pl.ds(i * 8 + n, 1), :] = state_ref[pl.ds(cell, 1), :]


def gather(ensemble, cells, tiles):
    members = ensemble.shape[-1]
    flat = ensemble.reshape(-1, members)
    count, nobs = cells.shape
    out = jax.ShapeDtypeStruct((2, count, nobs // 4, members), F32)
    return pl.pallas_call(
        gather_kernel,
        out_shape=[out, out],
        in_specs=[HBM] * 3,
        out_specs=[VMEM] * 2,
        scratch_shapes=[
            pltpu.SMEM(cells.shape, jnp.int32),
            pltpu.SMEM(tiles.shape[::-1], jnp.int32),
            pltpu.VMEM(flat.shape, F32),
            pltpu.SemaphoreType.DMA((3,)),
        ],
        compiler_params=pltpu.CompilerParams(vmem_limit_bytes=24 << 20),
    )(*map(in_hbm, (cells, tiles.T, flat)))


def spread_out(a, b, fillers):
    lon, lat = stages("lon", 2), stages("lat", 1)
    hops, made = list(zip(lon + lat, lat + lon)), []
    for n, ((a_axis, a_flip), (b_axis, b_flip)) in enumerate(hops):
        a_moved, b_moved = shifted(a, a_axis, a_flip), shifted(b, b_axis, b_flip)
        filler = fillers[n] if n < len(fillers) else None
        if filler is not None:
            function, args = filler
            args = args(made) if callable(args) else args
            a, b, args = lax.optimization_barrier((a, b, args))
            made.append(function(*args))
        a, b = a + a_moved, b + b_moved
        if filler is not None and n:
            a, b, made[n] = lax.optimization_barrier((a, b, made[n]))
    return (a, b, shifted(a, "lon", 1), shifted(b, "lon", 1)), made


def taper(lat_a, lon_a, lat_b, lon_b, radius, total_lon):
    lat_gap = (lat_a[:, None] - lat_b[None, :]).astype(F32)
    lon_gap = jnp.abs(lon_a[:, None] - lon_b[None, :])
    lon_gap = jnp.minimum(lon_gap, total_lon - lon_gap).astype(F32)
    radius = radius.astype(F32)
    ratio = 1.0 - (jnp.square(lat_gap) + jnp.square(lon_gap)) / (radius * radius)
    return jnp.square(jnp.maximum(ratio, 0.0))


def split(x):
    high = x.astype(BF16)
    return high, (x - high.astype(F32)).astype(BF16)


def exact_dot(a, b):
    return jnp.dot(a, b, precision=lax.Precision.HIGHEST, preferred_element_type=F32)


def split_dot(a, b_high, *b_rest):
    high, low = split(a)
    dot = functools.partial(jnp.dot, preferred_element_type=F32)
    total = dot(high, b_high) + dot(low, b_high)
    for b in b_rest:
        total = total + dot(high, b)
    return total


def lane_spread(x, lane):
    return jnp.take_along_axis(x, jnp.full(x.shape, lane, jnp.int32), axis=1)


def panel(strips):
    strips, shape = list(strips), strips[0].shape
    lane = lax.broadcasted_iota(jnp.int32, shape, 1)
    row = lax.broadcasted_iota(jnp.int32, shape, 0)
    for g, first in enumerate(strips):
        at = 8 * g
        block = jnp.logical_and(lane >= at, lane < at + 8)
        first = strips[g]
        diag = [lane_spread(first, at + c) for c in range(8)]
        left = {
            h: [lane_spread(strip, at + c) for c in range(8)]
            for h, strip in enumerate(strips)
            if h != g
        }
        scaled = jnp.where(block, jnp.where(lane == row + at, 1.0, 0.0), first)
        for k in range(0, 8, 2):

            def pick(x, n):
                return jnp.broadcast_to(x[n : n + 1], shape)

            p, q, r = pick(diag[k], k), pick(diag[k], k + 1), pick(diag[k + 1], k + 1)
            pivot = 1.0 / (p * r - q * q)

            def reduced(x):
                upper, lower = pick(x, k), pick(x, k + 1)
                upper, lower = (r * upper - q * lower) * pivot, (p * lower - q * upper) * pivot
                x = x - (diag[k] * upper + diag[k + 1] * lower)
                return jnp.where(row == k, upper, jnp.where(row == k + 1, lower, x))

            diag[k + 2 :] = [reduced(x) for x in diag[k + 2 :]]
            scaled = reduced(scaled)
        rows = [jnp.broadcast_to(scaled[c : c + 1], shape) for c in range(8)]
        for h, columns in left.items():
            terms = [columns[c] * rows[c] for c in range(8)]
            while len(terms) > 1:
                terms = [terms[j] + terms[j + 1] for j in range(0, len(terms), 2)]
            strips[h] = jnp.where(block, 0.0, strips[h]) - terms[0]
        strips[g] = scaled
    return strips


def inverse(a, block=64):
    size = a.shape[0]

    def turn(_, a):
        top = panel([a[8 * i : 8 * i + 8] for i in range(block // 8)])
        top, rest = jnp.concatenate(top), a[block:]
        lane = lax.broadcasted_iota(jnp.int32, rest.shape, 1)
        rest = jnp.where(lane < block, 0.0, rest) - exact_dot(rest[:, :block], top)
        return pltpu.roll(jnp.concatenate([rest, top]), size - block, 1)

    return lax.fori_loop(0, size // block, turn, a)


def solve_kernel(*refs):
    pieces, refs = refs[:4], refs[4:]
    target_ref, var_ref, mutual_ref, out_hbm, y_ref, out_ref, sem = refs
    count, nobs, members = target_ref.shape
    half = nobs // 2
    for n, piece in enumerate(pieces):
        size = piece.shape[1]
        y_ref[:, n * size : (n + 1) * size] = piece[...]
    diagonal = lax.broadcasted_iota(jnp.int32, (nobs, nobs), 0) == lax.broadcasted_iota(
        jnp.int32, (nobs, nobs), 1
    )

    @pl.loop(0, count)
    def _(b):
        y = y_ref[b]
        spread = y - jnp.sum(y, axis=1, keepdims=True) / members
        spread_t = spread.T
        out_ref[b, 0], out_ref[b, 1] = split(spread_t)
        cov = exact_dot(spread, spread_t) / (members - 1)
        cov = cov + jnp.where(diagonal, jnp.broadcast_to(var_ref[b], (nobs, nobs)), 0.0)
        right = target_ref[b] - y
        lower = cov[half:, :half]
        upper = jnp.concatenate([cov[:half, half:], right[:half]], axis=1)
        upper = exact_dot(inverse(cov[:half, :half]), upper)
        rest = exact_dot(lower, upper)
        schur = inverse(cov[half:, half:] - rest[:, :half])
        w_second = exact_dot(schur, right[half:] - rest[:, half:])
        w_first = upper[:, half:] - exact_dot(upper[:, :half], w_second)
        w = jnp.concatenate([w_first, w_second], axis=0)
        high, mid = split(w)
        out_ref[b, 2] = high
        out_ref[b, 3] = mid
        out_ref[b, 4] = (w - high.astype(F32) - mid.astype(F32)).astype(BF16)
        pltpu.make_async_copy(out_ref.at[b], out_hbm.at[b], sem).start()

        @pl.loop(b + 1, count)
        def _(later):
            y_later = y_ref[later]
            gain = exact_dot(y_later, spread_t) * mutual_ref[b + later - 1]
            y_ref[later] = y_later + exact_dot(gain, w)

    pltpu.make_async_copy(out_ref, out_hbm, sem).wait()


def solve(pieces, target, variance, mutual):
    count, nobs, members = target.shape
    out = (count, 5, nobs, members)
    return pl.pallas_call(
        solve_kernel,
        out_shape=jax.ShapeDtypeStruct(out, BF16),
        in_specs=[VMEM] * 7,
        out_specs=HBM,
        scratch_shapes=[
            pltpu.VMEM((count, nobs, members), F32),
            pltpu.VMEM(out, BF16),
            pltpu.SemaphoreType.DMA,
        ],
        compiler_params=pltpu.CompilerParams(vmem_limit_bytes=40 << 20),
        cost_estimate=pl.CostEstimate(
            flops=60 * count * nobs**3, bytes_accessed=4 * 8 * target.size, transcendentals=0
        ),
    )(*pieces, target, variance[:, None, :], mutual)


def sweep(source, j, height, coef_at, store):
    middle = [source[i, j + 1] for i in range(height + 2)]
    for i in range(height):
        near = (middle[i + 1], middle[i], middle[i + 2], source[i + 1, j], source[i + 1, j + 2])
        total = None
        for coef, part in zip(coef_at(i), near):
            coef = jnp.concatenate([coef] * (part.shape[-1] // coef.shape[-1]), axis=-1)
            total = part * coef if total is None else total + part * coef
        store(i, total)


def five(lat_speed, lon_speed, rate):
    return (
        1.0 - jnp.abs(lat_speed) - jnp.abs(lon_speed) - 4.0 * rate,
        jnp.maximum(lat_speed, 0.0) + rate,
        rate - jnp.minimum(lat_speed, 0.0),
        jnp.maximum(lon_speed, 0.0) + rate,
        rate - jnp.minimum(lon_speed, 0.0),
    )


def move_kernel(chunk, *refs):
    pieces, refs = refs[:5], refs[5:]
    taper_hbm, coef_hbm, factor_hbm, out_hbm, x_ref, taper_ref, factor_ref = refs[:7]
    coef_ref, wide_ref, z_ref, out_ref, sems, out_sem = refs[7:]
    count = factor_ref.shape[0]
    tall, wide, levels, members = x_ref.shape
    span = wide - 2 * HALO
    inner = pl.ds(HALO, span)
    moves = [(pieces[0], x_ref.at[pl.ds(HALO, tall - 2 * HALO), inner])]
    for n in range(HALO):
        rows = pl.ds(n * span, span)
        moves.append((pieces[1].at[rows], x_ref.at[n, inner]))
        moves.append((pieces[2].at[rows], x_ref.at[tall - HALO + n, inner]))
    for n in range(2):
        to = x_ref.at[:, pl.ds(n * (wide - HALO), HALO)]
        moves.append((pieces[3 + n].at[pl.ds(0, tall)], to))
    moves += [(taper_hbm, taper_ref), (factor_hbm, factor_ref)]
    moves.append((coef_hbm, coef_ref.at[:, pl.ds(1, wide - 4)]))
    for n in range(3):
        for side in range(2):
            source = pieces[3 + side].at[tall + n // 2, n % 2, :, pl.ds(0, coef_ref.shape[-1])]
            moves.append((source, coef_ref.at[n, side * (wide - 3)]))
    copies = [pltpu.make_async_copy(x, to, sems.at[n]) for n, (x, to) in enumerate(moves)]
    for copy in copies:
        copy.start()
    for copy in copies:
        copy.wait()

    columns = -(-(wide - 2) * chunk // tall)

    @pl.loop(0, tall // chunk)
    def _(i):
        at = pl.ds(i * chunk, chunk)
        x = x_ref[at].reshape(chunk * wide * levels, members)
        for b in range(count):
            gain = split_dot(x, factor_ref[b, 0], factor_ref[b, 1])
            gain = gain.reshape(chunk * wide, levels, -1)
            gain = gain * taper_ref[b, at].reshape(chunk * wide, -1)[:, None, :]
            gain = gain.reshape(chunk * wide * levels, -1)
            x = x + split_dot(gain, factor_ref[b, 2], factor_ref[b, 3], factor_ref[b, 4])
        x_ref[at] = x.reshape(chunk, wide, levels, members)
        for n in range(columns):
            j = jnp.minimum(i * columns + n, wide - 3)
            tiles = [coef_ref[kind, j] for kind in range(3)]
            for row in range(tall - 2):
                for kind, coef in enumerate(five(*[lane_spread(t, row) for t in tiles])):
                    wide_ref[kind, row, j] = coef

    @pl.loop(0, wide - 2)
    def _(j):
        def coef_at(i):
            return [wide_ref[n, i, j] for n in range(5)]

        def store(i, value):
            z_ref[i, j] = value

        sweep(x_ref, j, tall - 2, coef_at, store)

    @pl.loop(0, wide - 4)
    def _(j):
        def store(i, value):
            out_ref[i, j] = value

        def coef_at(i):
            return [wide_ref[n, i + 1, j + 1] for n in range(5)]

        sweep(z_ref, j, tall - 4, coef_at, store)
        pltpu.make_async_copy(out_ref.at[:, j], out_hbm.at[:, j], out_sem).start()

    pltpu.make_async_copy(out_ref, out_hbm, out_sem).wait()


def move(pieces, tapers, coefs, factors):
    tall, wide = pieces[0].shape[0] + 2 * HALO, pieces[0].shape[1] + 2 * HALO
    levels, members = pieces[0].shape[2:]
    return pl.pallas_call(
        functools.partial(move_kernel, 12 if tall % 12 == 0 else 1),
        out_shape=jax.ShapeDtypeStruct(pieces[0].shape, F32),
        in_specs=[HBM] * 8,
        out_specs=HBM,
        scratch_shapes=[
            pltpu.VMEM((tall, wide, levels, members), F32),
            pltpu.VMEM(tapers.shape, F32),
            pltpu.VMEM(factors.shape, BF16),
            pltpu.VMEM((3, wide - 2, levels, coefs.shape[-1]), F32),
            pltpu.VMEM((5, tall - 2, wide - 2, levels, LANES), F32),
            pltpu.VMEM((tall - 2, wide - 2, levels, members), F32),
            pltpu.VMEM(pieces[0].shape, F32),
            pltpu.SemaphoreType.DMA((10 + 2 * HALO + 6,)),
            pltpu.SemaphoreType.DMA,
        ],
        compiler_params=pltpu.CompilerParams(vmem_limit_bytes=60 << 20),
    )(*map(in_hbm, (*pieces, tapers, coefs, factors)))


def lanes(x, count):
    return jnp.pad(x, [(0, 0)] * (x.ndim - 1) + [(0, count - x.shape[-1])])


def neighbours(before, after, axis, wrap):
    size = lax.axis_size(axis)
    up = [(i, (i + 1) % size) for i in range(size if wrap else size - 1)]
    down = [(j, i) for i, j in up]
    return lax.ppermute(before, axis, up), lax.ppermute(after, axis, down)


def shards(
    ensemble,
    obs_values,
    obs_noise,
    obs_var,
    obs_cells,
    owner_tiles,
    radius,
    courant_lat,
    courant_lon,
    diffusivity,
):
    lat_index = lax.axis_index("lat")
    lon_index = lax.axis_index("lon")
    total_lon = CLON * lax.axis_size("lon")
    levels, members = ensemble.shape[2:]
    nobs = obs_cells.shape[1]

    core = lon_index % 2
    half = nobs // 2
    mine, others = gather(ensemble, obs_cells, owner_tiles)
    others = shifted(others, "lon", 1)
    a, b = mine[0] + others[0], mine[1] + others[1]
    def own_first(x):
        x = jnp.concatenate([x, x[:, :half]], axis=1)
        return lax.dynamic_slice_in_dim(x, core * half, nobs, 1)

    def lat_edges(ensemble, *speeds):
        speeds = jnp.stack(speeds).transpose(0, 2, 3, 1)

        def with_thin(edge, thin):
            thin = lanes(thin.transpose(2, 0, 1).reshape(levels, -1), members)
            return jnp.concatenate([edge.reshape((-1,) + edge.shape[2:]), thin[None]])

        south = with_thin(ensemble[-HALO:], speeds[..., -1])
        north = with_thin(ensemble[:HALO], speeds[..., 0])
        return speeds, *neighbours(south, north, "lat", False)

    tall, wide = ensemble.shape[0] + 2 * HALO, ensemble.shape[1] + 2 * HALO

    def obs_places(cells, tiles):
        place = own_first(cells) // levels
        return tiles[:, :1] * CLAT + place // CLON, tiles[:, 1:] * CLON + place % CLON

    def cell_tapers(cells, tiles, radius):
        obs_lat, obs_lon = obs_places(cells, tiles)
        lat_cells = lat_index * CLAT - HALO + jnp.arange(tall, dtype=jnp.int32)
        lon_cells = lon_index * CLON - HALO + jnp.arange(wide, dtype=jnp.int32)
        lon_cells = (lon_cells + total_lon) % total_lon
        lat_cells = jnp.broadcast_to(lat_cells[:, None], (tall, wide)).reshape(-1)
        lon_cells = jnp.broadcast_to(lon_cells[None, :], (tall, wide)).reshape(-1)
        tapers = [
            taper(lat_cells, lon_cells, obs_lat[b], obs_lon[b], radius[b], total_lon)
            for b in range(NBATCH)
        ]
        return jnp.stack(tapers).reshape(NBATCH, tall, wide, nobs) / (members - 1)

    def lon_edges(ensemble, speeds, south, north):
        def thin_of(side):
            thin = side[-1, :, : 3 * ensemble.shape[1]].reshape(levels, 3, -1)
            return thin.transpose(1, 2, 0)[..., None]

        speeds = jnp.concatenate([thin_of(south), speeds, thin_of(north)], axis=-1)
        speeds = lanes(speeds, LANES)
        shape = (HALO,) + ensemble.shape[1:]
        rows = (south[:-1].reshape(shape), ensemble, north[:-1].reshape(shape))

        def side(at, extent, lane):
            edge = jnp.concatenate([part[:, at:extent] for part in rows])
            tile = lanes(speeds[:, lane], members)
            tile = jnp.pad(tile, ((0, 1), (0, 0), (0, 0))).reshape((2, 2) + tile.shape[1:])
            return jnp.concatenate([edge, tile])

        last = ensemble.shape[1]
        return speeds, side(last - HALO, last, last - 1), side(0, HALO, 0)

    def obs_terms(cells, tiles, radius, values, noise, variance):
        obs_lat, obs_lon = obs_places(cells, tiles)
        mutual = [
            taper(obs_lat[c], obs_lon[c], obs_lat[b], obs_lon[b], radius[b], total_lon)
            for b, c in ((0, 1), (0, 2), (1, 2))
        ]
        values, noise, variance = map(own_first, (values, noise, variance))
        target = values[:, :, None] + jnp.sqrt(variance)[:, :, None] * noise
        return target, variance, jnp.stack(mutual) / (members - 1)

    pieces, made = spread_out(
        a,
        b,
        (
            (lat_edges, (ensemble, courant_lat, courant_lon, diffusivity)),
            (cell_tapers, (obs_cells, owner_tiles, radius)),
            (lon_edges, lambda made: (ensemble, *made[0])),
            (obs_terms, (obs_cells, owner_tiles, radius, obs_values, obs_noise, obs_var)),
        ),
    )
    (_, south, north), tapers, (speeds, before, after), (target, variance, mutual) = made
    west, east = neighbours(before, after, "lon", True)
    factors = solve(pieces, target, variance, mutual)
    cells = (ensemble, south, north, west, east)
    return move(cells, tapers, speeds, factors)


def solution(mesh):
    cells = P("lat", "lon", None)
    in_specs = (P("lat", "lon", None, None),) + (P(),) * 6 + (cells,) * 3
    out_specs = P("lat", "lon", None, None)
    return jax.shard_map(
        shards, mesh=mesh, in_specs=in_specs, out_specs=out_specs, check_vma=False
    )
```

```python
import functools

import jax
import jax.numpy as jnp
from jax import lax
from jax.experimental import pallas as pl
from jax.experimental.pallas import tpu as pltpu
from jax.sharding import PartitionSpec as P

NBATCH = 3
CLAT = 32
CLON = 16
HALO = 2
LANES = 128
F32 = jnp.float32
BF16 = jnp.bfloat16
VMEM = pl.BlockSpec(memory_space=pltpu.VMEM)
HBM = pl.BlockSpec(memory_space=pltpu.HBM)


def in_hbm(x):
    return pltpu.with_memory_space_constraint(x, pltpu.HBM)


def shifted(x, axis, flip):
    size = lax.axis_size(axis)
    return lax.ppermute(x, axis, [(i, i ^ flip) for i in range(size)])


def stages(axis, first):
    size, out = lax.axis_size(axis), []
    while first < size:
        out.append((axis, first))
        first *= 2
    return out


def gather_kernel(cells_hbm, tiles_hbm, state_hbm, *refs):
    first_ref, second_ref, cells, tiles, state_ref, sems = refs
    pairs = ((tiles_hbm, tiles), (cells_hbm, cells), (state_hbm, state_ref))
    copies = [pltpu.make_async_copy(x, to, sems.at[n]) for n, (x, to) in enumerate(pairs)]
    for copy in copies:
        copy.start()
    parts, count, rows, members = first_ref.shape
    lat, lon = lax.axis_index("lat"), lax.axis_index("lon")
    core = lax.rem(lon, 2)
    first_ref[...] = jnp.zeros(first_ref.shape, F32)
    second_ref[...] = jnp.zeros(second_ref.shape, F32)
    for copy in copies:
        copy.wait()
    for b in range(count):

        @pl.when(jnp.logical_and(tiles[0, b] == lat, tiles[1, b] == lon))
        def _():
            for side, ref in enumerate((first_ref, second_ref)):
                for part in range(parts):
                    start = (lax.rem(core + side, 2) * parts + part) * rows

                    @pl.loop(0, rows // 8)
                    def _(i):
                        for n in range(8):
                            cell = cells[b, start + i * 8 + n]
                            ref[part, b, pl.ds(i * 8 + n, 1), :] = state_ref[pl.ds(cell, 1), :]


def gather(ensemble, cells, tiles):
    members = ensemble.shape[-1]
    flat = ensemble.reshape(-1, members)
    count, nobs = cells.shape
    out = jax.ShapeDtypeStruct((2, count, nobs // 4, members), F32)
    return pl.pallas_call(
        gather_kernel,
        out_shape=[out, out],
        in_specs=[HBM] * 3,
        out_specs=[VMEM] * 2,
        scratch_shapes=[
            pltpu.SMEM(cells.shape, jnp.int32),
            pltpu.SMEM(tiles.shape[::-1], jnp.int32),
            pltpu.VMEM(flat.shape, F32),
            pltpu.SemaphoreType.DMA((3,)),
        ],
        compiler_params=pltpu.CompilerParams(vmem_limit_bytes=24 << 20),
    )(*map(in_hbm, (cells, tiles.T, flat)))


def spread_out(a, b, fillers):
    lon, lat = stages("lon", 2), stages("lat", 1)
    hops, made = list(zip(lon + lat, lat + lon)), []
    for n, ((a_axis, a_flip), (b_axis, b_flip)) in enumerate(hops):
        a_moved, b_moved = shifted(a, a_axis, a_flip), shifted(b, b_axis, b_flip)
        filler = fillers[n] if n < len(fillers) else None
        if filler is not None:
            function, args = filler
            args = args(made) if callable(args) else args
            a, b, args = lax.optimization_barrier((a, b, args))
            made.append(function(*args))
        a, b = a + a_moved, b + b_moved
        if filler is not None and n:
            a, b, made[n] = lax.optimization_barrier((a, b, made[n]))
    return (a, b, shifted(a, "lon", 1), shifted(b, "lon", 1)), made


def taper(lat_a, lon_a, lat_b, lon_b, radius, total_lon):
    lat_gap = (lat_a[:, None] - lat_b[None, :]).astype(F32)
    lon_gap = jnp.abs(lon_a[:, None] - lon_b[None, :])
    lon_gap = jnp.minimum(lon_gap, total_lon - lon_gap).astype(F32)
    radius = radius.astype(F32)
    ratio = 1.0 - (jnp.square(lat_gap) + jnp.square(lon_gap)) / (radius * radius)
    return jnp.square(jnp.maximum(ratio, 0.0))


def split(x):
    high = x.astype(BF16)
    return high, (x - high.astype(F32)).astype(BF16)


def exact_dot(a, b):
    return jnp.dot(a, b, precision=lax.Precision.HIGHEST, preferred_element_type=F32)


def split_dot(a, b_high, *b_rest):
    high, low = split(a)
    dot = functools.partial(jnp.dot, preferred_element_type=F32)
    total = dot(high, b_high) + dot(low, b_high)
    for b in b_rest:
        total = total + dot(high, b)
    return total


def lane_spread(x, lane):
    return jnp.take_along_axis(x, jnp.full(x.shape, lane, jnp.int32), axis=1)


def panel(strips):
    strips, shape = list(strips), strips[0].shape
    lane = lax.broadcasted_iota(jnp.int32, shape, 1)
    row = lax.broadcasted_iota(jnp.int32, shape, 0)
    for g, first in enumerate(strips):
        at = 8 * g
        block = jnp.logical_and(lane >= at, lane < at + 8)
        first = strips[g]
        diag = [lane_spread(first, at + c) for c in range(8)]
        left = {
            h: [lane_spread(strip, at + c) for c in range(8)]
            for h, strip in enumerate(strips)
            if h != g
        }
        scaled = jnp.where(block, jnp.where(lane == row + at, 1.0, 0.0), first)
        for k in range(0, 8, 2):

            def pick(x, n):
                return jnp.broadcast_to(x[n : n + 1], shape)

            p, q, r = pick(diag[k], k), pick(diag[k], k + 1), pick(diag[k + 1], k + 1)
            pivot = 1.0 / (p * r - q * q)

            def reduced(x):
                upper, lower = pick(x, k), pick(x, k + 1)
                upper, lower = (r * upper - q * lower) * pivot, (p * lower - q * upper) * pivot
                x = x - (diag[k] * upper + diag[k + 1] * lower)
                return jnp.where(row == k, upper, jnp.where(row == k + 1, lower, x))

            diag[k + 2 :] = [reduced(x) for x in diag[k + 2 :]]
            scaled = reduced(scaled)
        rows = [jnp.broadcast_to(scaled[c : c + 1], shape) for c in range(8)]
        for h, columns in left.items():
            terms = [columns[c] * rows[c] for c in range(8)]
            while len(terms) > 1:
                terms = [terms[j] + terms[j + 1] for j in range(0, len(terms), 2)]
            strips[h] = jnp.where(block, 0.0, strips[h]) - terms[0]
        strips[g] = scaled
    return strips


def inverse(a, block=64):
    size = a.shape[0]

    def turn(_, a):
        top = panel([a[8 * i : 8 * i + 8] for i in range(block // 8)])
        top, rest = jnp.concatenate(top), a[block:]
        lane = lax.broadcasted_iota(jnp.int32, rest.shape, 1)
        rest = jnp.where(lane < block, 0.0, rest) - exact_dot(rest[:, :block], top)
        return pltpu.roll(jnp.concatenate([rest, top]), size - block, 1)

    return lax.fori_loop(0, size // block, turn, a)


def solve_kernel(*refs):
    pieces, refs = refs[:4], refs[4:]
    target_ref, var_ref, mutual_ref, out_hbm, y_ref, out_ref, sem = refs
    count, nobs, members = target_ref.shape
    half = nobs // 2
    for n, piece in enumerate(pieces):
        size = piece.shape[1]
        y_ref[:, n * size : (n + 1) * size] = piece[...]
    diagonal = lax.broadcasted_iota(jnp.int32, (nobs, nobs), 0) == lax.broadcasted_iota(
        jnp.int32, (nobs, nobs), 1
    )

    @pl.loop(0, count)
    def _(b):
        y = y_ref[b]
        spread = y - jnp.sum(y, axis=1, keepdims=True) / members
        spread_t = spread.T
        out_ref[b, 0], out_ref[b, 1] = split(spread_t)
        cov = exact_dot(spread, spread_t) / (members - 1)
        cov = cov + jnp.where(diagonal, jnp.broadcast_to(var_ref[b], (nobs, nobs)), 0.0)
        right = target_ref[b] - y
        lower = cov[half:, :half]
        upper = jnp.concatenate([cov[:half, half:], right[:half]], axis=1)
        upper = exact_dot(inverse(cov[:half, :half]), upper)
        rest = exact_dot(lower, upper)
        schur = inverse(cov[half:, half:] - rest[:, :half])
        w_second = exact_dot(schur, right[half:] - rest[:, half:])
        w_first = upper[:, half:] - exact_dot(upper[:, :half], w_second)
        w = jnp.concatenate([w_first, w_second], axis=0)
        high, mid = split(w)
        out_ref[b, 2] = high
        out_ref[b, 3] = mid
        out_ref[b, 4] = (w - high.astype(F32) - mid.astype(F32)).astype(BF16)
        pltpu.make_async_copy(out_ref.at[b], out_hbm.at[b], sem).start()

        @pl.loop(b + 1, count)
        def _(later):
            y_later = y_ref[later]
            gain = exact_dot(y_later, spread_t) * mutual_ref[b + later - 1]
            y_ref[later] = y_later + exact_dot(gain, w)

    pltpu.make_async_copy(out_ref, out_hbm, sem).wait()


def solve(pieces, target, variance, mutual):
    count, nobs, members = target.shape
    out = (count, 5, nobs, members)
    return pl.pallas_call(
        solve_kernel,
        out_shape=jax.ShapeDtypeStruct(out, BF16),
        in_specs=[VMEM] * 7,
        out_specs=HBM,
        scratch_shapes=[
            pltpu.VMEM((count, nobs, members), F32),
            pltpu.VMEM(out, BF16),
            pltpu.SemaphoreType.DMA,
        ],
        compiler_params=pltpu.CompilerParams(vmem_limit_bytes=40 << 20),
        cost_estimate=pl.CostEstimate(
            flops=60 * count * nobs**3, bytes_accessed=4 * 8 * target.size, transcendentals=0
        ),
    )(*pieces, target, variance[:, None, :], mutual)


def sweep(source, j, height, coef_at, store):
    middle = [source[i, j + 1] for i in range(height + 2)]
    for i in range(height):
        near = (middle[i + 1], middle[i], middle[i + 2], source[i + 1, j], source[i + 1, j + 2])
        total = None
        for coef, part in zip(coef_at(i), near):
            coef = jnp.concatenate([coef] * (part.shape[-1] // coef.shape[-1]), axis=-1)
            total = part * coef if total is None else total + part * coef
        store(i, total)


def five(lat_speed, lon_speed, rate):
    return (
        1.0 - jnp.abs(lat_speed) - jnp.abs(lon_speed) - 4.0 * rate,
        jnp.maximum(lat_speed, 0.0) + rate,
        rate - jnp.minimum(lat_speed, 0.0),
        jnp.maximum(lon_speed, 0.0) + rate,
        rate - jnp.minimum(lon_speed, 0.0),
    )


def move_kernel(chunk, *refs):
    pieces, refs = refs[:5], refs[5:]
    taper_hbm, coef_hbm, factor_hbm, out_hbm, x_ref, taper_ref, factor_ref = refs[:7]
    coef_ref, wide_ref, z_ref, out_ref, sems, out_sem = refs[7:]
    count = factor_ref.shape[0]
    tall, wide, levels, members = x_ref.shape
    span = wide - 2 * HALO
    inner = pl.ds(HALO, span)
    moves = [(pieces[0], x_ref.at[pl.ds(HALO, tall - 2 * HALO), inner])]
    for n in range(HALO):
        rows = pl.ds(n * span, span)
        moves.append((pieces[1].at[rows], x_ref.at[n, inner]))
        moves.append((pieces[2].at[rows], x_ref.at[tall - HALO + n, inner]))
    for n in range(2):
        to = x_ref.at[:, pl.ds(n * (wide - HALO), HALO)]
        moves.append((pieces[3 + n].at[pl.ds(0, tall)], to))
    moves += [(taper_hbm, taper_ref), (factor_hbm, factor_ref)]
    moves.append((coef_hbm, coef_ref.at[:, pl.ds(1, wide - 4)]))
    for n in range(3):
        for side in range(2):
            source = pieces[3 + side].at[tall + n // 2, n % 2, :, pl.ds(0, coef_ref.shape[-1])]
            moves.append((source, coef_ref.at[n, side * (wide - 3)]))
    copies = [pltpu.make_async_copy(x, to, sems.at[n]) for n, (x, to) in enumerate(moves)]
    for copy in copies:
        copy.start()
    for copy in copies:
        copy.wait()

    columns = -(-(wide - 2) * chunk // tall)

    @pl.loop(0, tall // chunk)
    def _(i):
        at = pl.ds(i * chunk, chunk)
        x = x_ref[at].reshape(chunk * wide * levels, members)
        for b in range(count):
            gain = split_dot(x, factor_ref[b, 0], factor_ref[b, 1])
            gain = gain.reshape(chunk * wide, levels, -1)
            gain = gain * taper_ref[b, at].reshape(chunk * wide, -1)[:, None, :]
            gain = gain.reshape(chunk * wide * levels, -1)
            x = x + split_dot(gain, factor_ref[b, 2], factor_ref[b, 3], factor_ref[b, 4])
        x_ref[at] = x.reshape(chunk, wide, levels, members)
        for n in range(columns):
            j = jnp.minimum(i * columns + n, wide - 3)
            tiles = [coef_ref[kind, j] for kind in range(3)]
            for row in range(tall - 2):
                for kind, coef in enumerate(five(*[lane_spread(t, row) for t in tiles])):
                    wide_ref[kind, row, j] = coef

    @pl.loop(0, wide - 2)
    def _(j):
        def coef_at(i):
            return [wide_ref[n, i, j] for n in range(5)]

        def store(i, value):
            z_ref[i, j] = value

        sweep(x_ref, j, tall - 2, coef_at, store)

    @pl.loop(0, wide - 4)
    def _(j):
        def store(i, value):
            out_ref[i, j] = value

        def coef_at(i):
            return [wide_ref[n, i + 1, j + 1] for n in range(5)]

        sweep(z_ref, j, tall - 4, coef_at, store)
        pltpu.make_async_copy(out_ref.at[:, j], out_hbm.at[:, j], out_sem).start()

    pltpu.make_async_copy(out_ref, out_hbm, out_sem).wait()


def move(pieces, tapers, coefs, factors):
    tall, wide = pieces[0].shape[0] + 2 * HALO, pieces[0].shape[1] + 2 * HALO
    levels, members = pieces[0].shape[2:]
    return pl.pallas_call(
        functools.partial(move_kernel, 12 if tall % 12 == 0 else 1),
        out_shape=jax.ShapeDtypeStruct(pieces[0].shape, F32),
        in_specs=[HBM] * 8,
        out_specs=HBM,
        scratch_shapes=[
            pltpu.VMEM((tall, wide, levels, members), F32),
            pltpu.VMEM(tapers.shape, F32),
            pltpu.VMEM(factors.shape, BF16),
            pltpu.VMEM((3, wide - 2, levels, coefs.shape[-1]), F32),
            pltpu.VMEM((5, tall - 2, wide - 2, levels, LANES), F32),
            pltpu.VMEM((tall - 2, wide - 2, levels, members), F32),
            pltpu.VMEM(pieces[0].shape, F32),
            pltpu.SemaphoreType.DMA((10 + 2 * HALO + 6,)),
            pltpu.SemaphoreType.DMA,
        ],
        compiler_params=pltpu.CompilerParams(vmem_limit_bytes=50 << 20),
    )(*map(in_hbm, pieces[:3]), *pieces[3:], in_hbm(tapers), in_hbm(coefs), factors)


def lanes(x, count):
    return jnp.pad(x, [(0, 0)] * (x.ndim - 1) + [(0, count - x.shape[-1])])


def neighbours(before, after, axis, wrap):
    size = lax.axis_size(axis)
    up = [(i, (i + 1) % size) for i in range(size if wrap else size - 1)]
    down = [(j, i) for i, j in up]
    return lax.ppermute(before, axis, up), lax.ppermute(after, axis, down)


def shards(
    ensemble,
    obs_values,
    obs_noise,
    obs_var,
    obs_cells,
    owner_tiles,
    radius,
    courant_lat,
    courant_lon,
    diffusivity,
):
    lat_index = lax.axis_index("lat")
    lon_index = lax.axis_index("lon")
    total_lon = CLON * lax.axis_size("lon")
    levels, members = ensemble.shape[2:]
    nobs = obs_cells.shape[1]

    core = lon_index % 2
    half = nobs // 2
    mine, others = gather(ensemble, obs_cells, owner_tiles)
    others = shifted(others, "lon", 1)
    a, b = mine[0] + others[0], mine[1] + others[1]
    def own_first(x):
        x = jnp.concatenate([x, x[:, :half]], axis=1)
        return lax.dynamic_slice_in_dim(x, core * half, nobs, 1)

    def lat_edges(ensemble, *speeds):
        speeds = jnp.stack(speeds).transpose(0, 2, 3, 1)

        def with_thin(edge, thin):
            thin = lanes(thin.transpose(2, 0, 1).reshape(levels, -1), members)
            return jnp.concatenate([edge.reshape((-1,) + edge.shape[2:]), thin[None]])

        south = with_thin(ensemble[-HALO:], speeds[..., -1])
        north = with_thin(ensemble[:HALO], speeds[..., 0])
        return speeds, *neighbours(south, north, "lat", False)

    tall, wide = ensemble.shape[0] + 2 * HALO, ensemble.shape[1] + 2 * HALO

    def obs_places(cells, tiles):
        place = own_first(cells) // levels
        return tiles[:, :1] * CLAT + place // CLON, tiles[:, 1:] * CLON + place % CLON

    def cell_tapers(cells, tiles, radius):
        obs_lat, obs_lon = obs_places(cells, tiles)
        lat_cells = lat_index * CLAT - HALO + jnp.arange(tall, dtype=jnp.int32)
        lon_cells = lon_index * CLON - HALO + jnp.arange(wide, dtype=jnp.int32)
        lon_cells = (lon_cells + total_lon) % total_lon
        lat_cells = jnp.broadcast_to(lat_cells[:, None], (tall, wide)).reshape(-1)
        lon_cells = jnp.broadcast_to(lon_cells[None, :], (tall, wide)).reshape(-1)
        tapers = [
            taper(lat_cells, lon_cells, obs_lat[b], obs_lon[b], radius[b], total_lon)
            for b in range(NBATCH)
        ]
        return jnp.stack(tapers).reshape(NBATCH, tall, wide, nobs) / (members - 1)

    def lon_edges(ensemble, speeds, south, north):
        def thin_of(side):
            thin = side[-1, :, : 3 * ensemble.shape[1]].reshape(levels, 3, -1)
            return thin.transpose(1, 2, 0)[..., None]

        speeds = jnp.concatenate([thin_of(south), speeds, thin_of(north)], axis=-1)
        speeds = lanes(speeds, LANES)
        shape = (HALO,) + ensemble.shape[1:]
        rows = (south[:-1].reshape(shape), ensemble, north[:-1].reshape(shape))

        def side(at, extent, lane):
            edge = jnp.concatenate([part[:, at:extent] for part in rows])
            tile = lanes(speeds[:, lane], members)
            tile = jnp.pad(tile, ((0, 1), (0, 0), (0, 0))).reshape((2, 2) + tile.shape[1:])
            return jnp.concatenate([edge, tile])

        last = ensemble.shape[1]
        return speeds, side(last - HALO, last, last - 1), side(0, HALO, 0)

    def obs_terms(cells, tiles, radius, values, noise, variance):
        obs_lat, obs_lon = obs_places(cells, tiles)
        mutual = [
            taper(obs_lat[c], obs_lon[c], obs_lat[b], obs_lon[b], radius[b], total_lon)
            for b, c in ((0, 1), (0, 2), (1, 2))
        ]
        values, noise, variance = map(own_first, (values, noise, variance))
        target = values[:, :, None] + jnp.sqrt(variance)[:, :, None] * noise
        return target, variance, jnp.stack(mutual) / (members - 1)

    pieces, made = spread_out(
        a,
        b,
        (
            (lat_edges, (ensemble, courant_lat, courant_lon, diffusivity)),
            (cell_tapers, (obs_cells, owner_tiles, radius)),
            (lon_edges, lambda made: (ensemble, *made[0])),
            (obs_terms, (obs_cells, owner_tiles, radius, obs_values, obs_noise, obs_var)),
        ),
    )
    (_, south, north), tapers, (speeds, before, after), (target, variance, mutual) = made
    west, east = neighbours(before, after, "lon", True)
    factors = solve(pieces, target, variance, mutual)
    cells = (ensemble, south, north, west, east)
    return move(cells, tapers, speeds, factors)


def solution(mesh):
    cells = P("lat", "lon", None)
    in_specs = (P("lat", "lon", None, None),) + (P(),) * 6 + (cells,) * 3
    out_specs = P("lat", "lon", None, None)
    return jax.shard_map(
        shards, mesh=mesh, in_specs=in_specs, out_specs=out_specs, check_vma=False
    )
```
